32 devices in a mesh: grp: 4 (over x, core), blk: 8 (over z, y).
Axes of the slice: x: 2, y: 2, z: 4, core: 2. Of those that a mesh axis runs over, the one named last changes fastest.
Arguments:
- residual: float32 [3, 16, 128, 512], P(None, 'blk', None, 'grp'), may hold values from -8 to 8
- face_mask: int32 [3, 16, 128, 512], P(None, 'blk', None, 'grp'), may hold values 0 or 1
- conductivity: float32 [4, 16, 128, 512], P('grp', 'blk'), may hold values from 0.5 to 4
- stencil: float32 [4, 27, 3, 3], replicated, may hold values from -1.5 to 1.5, as said below
Outputs:
- correction: float32 [3, 16, 128, 512], P(None, 'blk', None, 'grp')
The draws below stay inside these ranges and needn't reach their ends.
Inputs may be any that keep to these rules, and one draw needn't show every extreme that they name: In each space's stencil the diagonal of the block at offset 0 exceeds the sum of magnitudes of all other entries of its row.
All inputs are finite; a program needn't handle non-finite values. No bound on the sum of `face_mask` on one device may be relied on, other than what follows from the above.
Results may differ from the reference program's by a relative error of at most 0.0001.
Values sent between devices are 32-bit elements; how exact they have to be, the bound alone decides.
A program may use at most 192 MiB of HBM per device.

```python
import math
import jax
import jax.numpy as jnp

NY = 128
NZ = 512
NX = 16


def draw_stencil(key, part):
    key_off = jax.random.fold_in(key, 11)
    key_diag = jax.random.fold_in(key, 12)
    key_cross = jax.random.fold_in(key, 13)
    offdiag = 0.01 * jax.random.normal(key_off, (4, 27, 3, 3), jnp.float32)
    diagonal = 1.0 + 0.5 * jax.random.uniform(key_diag, (4, 3), jnp.float32)
    cross = jnp.clip(0.1 * jax.random.normal(key_cross, (4, 3, 3), jnp.float32), -0.1, 0.1)
    identity = jnp.eye(3, dtype=jnp.float32)
    offdiag = jnp.clip(offdiag, -0.017, 0.017)
    centre = diagonal[:, :, None] * identity + cross * (1.0 - identity)
    return offdiag.at[:, 13].set(centre)


def place_ends(entries, rng, smallest, high):
    index_at = [jax.random.randint(jax.random.fold_in(rng, axis), (), 0, length) for axis, length in enumerate(entries.shape)]
    main_axis = entries.shape.index(max(entries.shape))
    beside = index_at[:main_axis] + [(index_at[main_axis] + 1) % entries.shape[main_axis]] + index_at[main_axis + 1:]
    return entries.at[tuple(index_at)].set(smallest).at[tuple(beside)].set(high)


def steps_of(key, dims, shards, smallest, largest):
    level, own = 1.0, jax.random.fold_in(key, 6)
    for position, parts in shards:
        draws = jnp.exp(jax.random.uniform(jax.random.fold_in(own, position), (parts,), jnp.float32, smallest / len(shards), largest / len(shards)))
        level = level * jnp.repeat(draws, dims[position] // parts).reshape([-1 if axis == position else 1 for axis in range(len(dims))])
    return level


def normal_values(stream_key, extent, scale, reach, shards=(), held_as=jnp.bfloat16):
    gain = steps_of(stream_key, extent, shards, -0.22, 0.18) if shards else 1.0
    array = jax.random.normal(stream_key, extent, jnp.float32) * scale * gain
    return jnp.minimum(jnp.maximum(array, -reach), reach).astype(held_as)


def setup_inputs(seed: int = 0) -> dict:
    key_of = jax.random.split(jax.random.key(seed), 5)
    return {
        "residual": normal_values(key_of[0], (3, NX, NY, NZ), 1.0, 8.0, ((1, 8), (3, 4)), jnp.float32),
        "face_mask": place_ends((jax.random.randint(key_of[1], (3, NX, NY, NZ), 0, 8) < 7).astype(jnp.int32), jax.random.fold_in(key_of[1], 1), 0, 1),
        "conductivity": jnp.clip(jnp.exp(math.log(4.0) - 2.0794415 * jax.random.uniform(key_of[2], (4, NX, NY, NZ), jnp.float32) ** steps_of(key_of[2], (4, NX, NY, NZ), ((0, 4), (1, 8)), -0.2, 0.2)), 0.5, 4.0),
        "stencil": draw_stencil(jax.random.fold_in(key_of[4], 71), 0),
    }


OMEGA = 0.8


def place_of(shift_x, shift_y, shift_z):
    return 9 * (shift_x + 1) + 3 * (shift_y + 1) + (shift_z + 1)


def blank_tables():
    return [[[[0.0, 0.0, 0.0] for row_one in range(3)] for place in range(27)] for space in range(4)]


def restriction_tables():
    forward = blank_tables()
    centre = place_of(0, 0, 0)
    for comp in range(3):
        forward[0][centre][comp][comp] = 1.0
        others = [axis_one for axis_one in range(3) if axis_one != comp]
        for first_off in (0, -1):
            for second_off in (0, -1):
                vector = [0, 0, 0]
                vector[others[0]] = first_off
                vector[others[1]] = second_off
                forward[1][place_of(*vector)][comp][comp] += 0.25
        along_p = (comp + 1) % 3
        along_q = (comp + 2) % 3
        forward[2][centre][comp][along_q] += 1.0
        forward[2][centre][comp][along_p] -= 1.0
        vector = [0, 0, 0]
        vector[along_p] = -1
        forward[2][place_of(*vector)][comp][along_q] -= 1.0
        vector = [0, 0, 0]
        vector[along_q] = -1
        forward[2][place_of(*vector)][comp][along_p] += 1.0
    for comp in range(3):
        for shift_x in (-1, 0, 1):
            for shift_y in (-1, 0, 1):
                for shift_z in (-1, 0, 1):
                    source = list(forward[2][place_of(shift_x, shift_y, shift_z)][comp])
                    if abs(source[0]) + abs(source[1]) + abs(source[2]) == 0:
                        continue
                    vector = [shift_x, shift_y, shift_z]
                    vector[comp] += 1
                    for column in range(3):
                        forward[3][place_of(shift_x, shift_y, shift_z)][comp][column] += 0.5 * source[column]
                        forward[3][place_of(*vector)][comp][column] += 0.5 * source[column]
    backward = blank_tables()
    for space in range(4):
        for shift_x in (-1, 0, 1):
            for shift_y in (-1, 0, 1):
                for shift_z in (-1, 0, 1):
                    for row_one in range(3):
                        for column in range(3):
                            backward[space][place_of(-shift_x, -shift_y, -shift_z)][row_one][column] = forward[space][place_of(shift_x, shift_y, shift_z)][column][row_one]
    return forward, backward


def stencil_apply(table, field):
    rows_x = field.shape[1] - 2
    rows_y = field.shape[2]
    rows_z = field.shape[3]
    padded = jnp.pad(field, ((0, 0), (0, 0), (1, 1), (1, 1)))
    total = jnp.zeros((3, rows_x, rows_y, rows_z), jnp.float32)
    for shift_x in (-1, 0, 1):
        for shift_y in (-1, 0, 1):
            for shift_z in (-1, 0, 1):
                piece = padded[:, 1 + shift_x:1 + shift_x + rows_x, 1 + shift_y:1 + shift_y + rows_y, 1 + shift_z:1 + shift_z + rows_z]
                block = table[place_of(shift_x, shift_y, shift_z)]
                total = total + (block[:, :, None, None, None] * piece[None]).sum(1)
    return total


def pad_first(field):
    return jnp.pad(field, ((0, 0), (1, 1), (0, 0), (0, 0)))


def reference(residual, face_mask, conductivity, stencil):
    mask_float = face_mask.astype(jnp.float32)
    masked = residual * mask_float
    forward, backward = restriction_tables()
    fwd_all = jnp.asarray(forward, jnp.float32)
    bwd_all = jnp.asarray(backward, jnp.float32)
    total = jnp.zeros(residual.shape, jnp.float32)
    for group in range(4):
        restricted = stencil_apply(fwd_all[group], pad_first(masked))
        centre = jnp.diagonal(stencil[group, 13])
        coeff = conductivity[group][None]
        scale = OMEGA / (coeff * centre[:, None, None, None])
        first = restricted * scale
        applied = coeff * stencil_apply(stencil[group], pad_first(first))
        second = first + (restricted - applied) * scale
        total = total + stencil_apply(bwd_all[group], pad_first(second))
    return total * mask_float
```

```python
import jax
import jax.numpy as jnp
from jax import lax
from jax.experimental import pallas as pl
from jax.experimental.pallas import tpu as pltpu
from jax.sharding import PartitionSpec as P

OMEGA = 0.8
PAD = 8


def place_of(shift_x, shift_y, shift_z):
    return 9 * (shift_x + 1) + 3 * (shift_y + 1) + (shift_z + 1)


def blank_tables():
    return [
        [[[0.0, 0.0, 0.0] for row_one in range(3)] for place in range(27)] for space in range(4)
    ]


def restriction_tables():
    forward = blank_tables()
    centre = place_of(0, 0, 0)
    for comp in range(3):
        forward[0][centre][comp][comp] = 1.0
        others = [axis_one for axis_one in range(3) if axis_one != comp]
        for first_off in (0, -1):
            for second_off in (0, -1):
                vector = [0, 0, 0]
                vector[others[0]] = first_off
                vector[others[1]] = second_off
                forward[1][place_of(*vector)][comp][comp] += 0.25
        along_p = (comp + 1) % 3
        along_q = (comp + 2) % 3
        forward[2][centre][comp][along_q] += 1.0
        forward[2][centre][comp][along_p] -= 1.0
        vector = [0, 0, 0]
        vector[along_p] = -1
        forward[2][place_of(*vector)][comp][along_q] -= 1.0
        vector = [0, 0, 0]
        vector[along_q] = -1
        forward[2][place_of(*vector)][comp][along_p] += 1.0
    for comp in range(3):
        for shift_x in (-1, 0, 1):
            for shift_y in (-1, 0, 1):
                for shift_z in (-1, 0, 1):
                    source = list(forward[2][place_of(shift_x, shift_y, shift_z)][comp])
                    if abs(source[0]) + abs(source[1]) + abs(source[2]) == 0:
                        continue
                    vector = [shift_x, shift_y, shift_z]
                    vector[comp] += 1
                    for column in range(3):
                        forward[3][place_of(shift_x, shift_y, shift_z)][comp][column] += (
                            0.5 * source[column]
                        )
                        forward[3][place_of(*vector)][comp][column] += 0.5 * source[column]
    backward = blank_tables()
    for space in range(4):
        for shift_x in (-1, 0, 1):
            for shift_y in (-1, 0, 1):
                for shift_z in (-1, 0, 1):
                    for row_one in range(3):
                        for column in range(3):
                            backward[space][place_of(-shift_x, -shift_y, -shift_z)][row_one][
                                column
                            ] = forward[space][place_of(shift_x, shift_y, shift_z)][column][row_one]
    return (forward, backward)


def terms_of(table):
    rows = [[] for comp in range(3)]
    for dx in (-1, 0, 1):
        for dy in (-1, 0, 1):
            for dz in (-1, 0, 1):
                for row in range(3):
                    for column in range(3):
                        weight = table[place_of(dx, dy, dz)][row][column]
                        if weight != 0.0:
                            rows[row].append((dx, dy, dz, column, weight))
    return rows


def weighted(terms, load):
    groups = {}
    for dx, dy, dz, column, weight in terms:
        piece = load(dx, dy, dz, column)
        held = groups.get(abs(weight))
        if held is None:
            groups[abs(weight)] = piece if weight > 0 else -piece
        else:
            groups[abs(weight)] = held + piece if weight > 0 else held - piece
    total = None
    for size, held in groups.items():
        held = held if size == 1.0 else held * size
        total = held if total is None else total + held
    return total


def ring(own, beside, step, lane):
    width = own.shape[-1]
    turn = 1 if step < 0 else width - 1
    edge = 0 if step < 0 else width - 1
    own_turned = pltpu.roll(own, turn, own.ndim - 1)
    beside_turned = pltpu.roll(beside, turn, own.ndim - 1)
    at_edge = lane == edge
    return (
        jnp.where(at_edge, beside_turned, own_turned),
        jnp.where(at_edge, own_turned, beside_turned),
    )


def compute(weights, inverse, m, mh, c, ch, mz, mhz, f, rs, inv, sec, b, edges, layers, tall):
    first_block, last_block, first_lanes, last_lanes = edges
    forward, backward = restriction_tables()
    rows = tall - 2 * PAD
    chunk = 16
    width = m.shape[-1]
    lane = lax.broadcasted_iota(jnp.int32, (chunk, width), 1)
    zeros = jnp.zeros((PAD, width), jnp.float32)
    count = rows // chunk

    def at(index, shift=0):
        return pl.ds(index * chunk + (PAD + shift), chunk)

    for side in (0, 1):
        edge = pl.ds(side * (rows + PAD), PAD)
        for layer in range(layers + 4):
            for comp in range(3):
                m[layer, comp, edge, :] = zeros
                mh[layer, comp, edge, :] = zeros
                for dz in (0, 1):
                    mz[dz, layer, comp, edge, :] = zeros
                    mhz[dz, layer, comp, edge, :] = zeros
        for comp in range(3):
            for layer in range(layers + 2):
                for dz in range(3):
                    f[dz, comp, layer, edge, :] = zeros
            for layer in range(layers):
                sec[comp, layer, edge, :] = zeros

    @pl.loop(0, (layers + 4) * 3)
    def _(plane):
        layer, comp = plane // 3, plane % 3

        @pl.loop(0, count)
        def _(i):
            own, beside = m[layer, comp, at(i), :], mh[layer, comp, at(i), :]
            for dz in (0, 1):
                one, other = ring(own, beside, 2 * dz - 1, lane)
                mz[dz, layer, comp, at(i), :] = one
                mhz[dz, layer, comp, at(i), :] = other

    for space in range(4):
        table = terms_of(forward[space])
        base = space * 243

        @pl.loop(0, layers + 2)
        def _(layer):
            off = jnp.logical_or(
                jnp.logical_and(first_block, layer == 0),
                jnp.logical_and(last_block, layer == layers + 1),
            )
            off_left = jnp.logical_or(off, first_lanes)
            off_right = jnp.logical_or(off, last_lanes)

            @pl.loop(0, count)
            def _(i):
                flat = pl.ds(i * chunk, chunk)
                scale = OMEGA / c[space, layer, flat, :]
                scale_h = OMEGA / ch[space, layer, flat, :]
                inv[layer, flat, :] = scale
                for comp in range(3):
                    def own(dx, dy, dz, column):
                        place = m if dz == 0 else mz.at[(dz + 1) // 2]
                        return place[layer + 1 + dx, column, at(i, dy), :]

                    def beside(dx, dy, dz, column):
                        place = mh if dz == 0 else mhz.at[(dz + 1) // 2]
                        return place[layer + 1 + dx, column, at(i, dy), :]

                    centre = inverse[space * 3 + comp]
                    restricted = weighted(table[comp], own)
                    rs[layer, comp, flat, :] = restricted
                    value = jnp.where(off, 0.0, restricted * (scale * centre))
                    value_h = weighted(table[comp], beside) * (scale_h * centre)
                    gone = jnp.where(lane == 0, off_right.astype(jnp.int32), off_left.astype(jnp.int32))
                    value_h = jnp.where(gone != 0, 0.0, value_h)
                    f[1, comp, layer, at(i), :] = value
                    f[0, comp, layer, at(i), :] = ring(value, value_h, -1, lane)[0]
                    f[2, comp, layer, at(i), :] = ring(value, value_h, 1, lane)[0]

        @pl.loop(0, count)
        def _(i):
            flat = pl.ds(i * chunk, chunk)
            total = [[None] * 3 for layer in range(layers)]
            for dy in (-1, 0, 1):
                for dz in (-1, 0, 1):
                    for column in range(3):
                        planes = [f[dz + 1, column, layer, at(i, dy), :] for layer in range(layers + 2)]
                        for dx in (-1, 0, 1):
                            for comp in range(3):
                                weight = weights[base + place_of(dx, dy, dz) * 9 + comp * 3 + column]
                                for layer in range(layers):
                                    piece = planes[layer + 1 + dx] * weight
                                    held = total[layer][comp]
                                    total[layer][comp] = piece if held is None else held + piece
            for layer in range(layers):
                scale = inv[layer + 1, flat, :]
                coeff = c[space, layer + 1, flat, :]
                for comp in range(3):
                    left = rs[layer + 1, comp, flat, :] - coeff * total[layer][comp]
                    value = f[1, comp, layer + 1, at(i), :]
                    sec[comp, layer, at(i), :] = value + left * (scale * inverse[space * 3 + comp])

        table = terms_of(backward[space])

        @pl.loop(0, count)
        def _(i):
            flat = pl.ds(i * chunk, chunk)
            for layer in range(layers + 2):
                for comp in range(3):
                    for dz in (-1, 0, 1):
                        terms = [
                            term
                            for term in table[comp]
                            if term[2] == dz and 0 <= layer - 1 + term[0] < layers
                        ]
                        if terms:
                            def load(dx, dy, dz, column):
                                return sec[column, layer - 1 + dx, at(i, dy), :]

                            value = weighted(terms, load)
                            if space > 0:
                                value = value + b[dz + 1, layer, comp, flat, :]
                            b[dz + 1, layer, comp, flat, :] = value
                        elif space == 0:
                            b[dz + 1, layer, comp, flat, :] = jnp.zeros((chunk, width), jnp.float32)


def finish(b, layers, rows, width, store):
    chunk = 16
    lane = lax.broadcasted_iota(jnp.int32, (chunk, width), 1)

    @pl.loop(0, (layers + 2) * 3)
    def _(plane):
        layer, comp = plane // 3, plane % 3

        @pl.loop(0, rows // chunk)
        def _(i):
            flat = pl.ds(i * chunk, chunk)
            before = pltpu.roll(b[0, layer, comp, flat, :], 1, 1)
            after = pltpu.roll(b[2, layer, comp, flat, :], width - 1, 1)
            own = b[1, layer, comp, flat, :]
            own = own + jnp.where(lane == 0, 0.0, before) + jnp.where(lane == width - 1, 0.0, after)
            store(layer, comp, flat, own, jnp.where(lane == 0, before, after))


def kernel(blocks, groups, weights, inverse, m_in, mh_in, c, ch, own_ref, out_ref, m, mh, mz, mhz, f, rs, inv, sec, b):
    layers, tall, width = m.shape[0] - 4, m.shape[2], m.shape[3]
    rows = tall - 2 * PAD
    block, group = lax.axis_index("blk"), lax.axis_index("grp")
    edges = (block == 0, block == blocks - 1, group == 0, group == groups - 1)

    @pl.loop(0, (layers + 4) * 3)
    def _(plane):
        layer, comp = plane // 3, plane % 3
        m[layer, comp, pl.ds(PAD, rows), :] = m_in[layer, comp]
        mh[layer, comp, pl.ds(PAD, rows), :] = mh_in[layer, comp]

    compute(weights, inverse, m, mh, c, ch, mz, mhz, f, rs, inv, sec, b, edges, layers, tall)

    def store(layer, comp, flat, own, outside):
        own_ref[layer, comp, flat, :] = own
        out_ref[layer, comp, flat, :] = outside

    finish(b, layers, rows, width, store)


def shift(value, axis, step):
    count = lax.axis_size(axis)
    pairs = [(i, i + step) for i in range(count) if 0 <= i + step < count]
    return lax.ppermute(value, axis, pairs)


def local(residual, face_mask, conductivity, stencil):
    groups, blocks = lax.axis_size("grp"), lax.axis_size("blk")
    mask_float = face_mask.astype(jnp.float32)
    masked = jnp.swapaxes(residual * mask_float, 0, 1)
    layers, _, rows, width = masked.shape
    tall = rows + 2 * PAD
    low = shift(jnp.concatenate([masked[layers - 2, 1:], masked[layers - 1]]), "blk", 1)
    high = shift(jnp.concatenate([masked[0], masked[1, 1:]]), "blk", -1)
    coeff = conductivity[0].reshape(layers, rows, groups, width)
    coeff = lax.all_to_all(coeff.transpose(2, 0, 1, 3), "grp", 0, 0)
    low_c = shift(coeff[:, layers - 1], "blk", 1)
    high_c = shift(coeff[:, 0], "blk", -1)
    nought = jnp.zeros((1, rows, width), jnp.float32)
    m = jnp.concatenate([nought, low[:2], low[2:], masked.reshape(-1, rows, width), high[:3], nought, high[3:]])
    c = jnp.concatenate([low_c[:, None], coeff, high_c[:, None]], 1)
    flat_c = c.reshape(-1, rows, width)
    planes = m.shape[0]
    right = shift(jnp.concatenate([m[..., width - 2], m[..., width - 1], flat_c[..., width - 1]]), "grp", 1)
    left = shift(jnp.concatenate([m[..., 0], m[..., 1], flat_c[..., 0]]), "grp", -1)
    gap = jnp.zeros((planes, rows, width - 4), jnp.float32)
    mh = jnp.concatenate(
        [left[:planes, :, None], left[planes : 2 * planes, :, None], gap, right[:planes, :, None], right[planes : 2 * planes, :, None]],
        2,
    )
    gap = jnp.ones((flat_c.shape[0], rows, width - 2), jnp.float32)
    ch = jnp.concatenate([left[2 * planes :, :, None], gap, right[2 * planes :, :, None]], 2)
    weights = stencil.reshape(-1)
    inverse = (1.0 / jnp.diagonal(stencil[:, 13], axis1=1, axis2=2)).reshape(-1)

    smem, vmem = pl.BlockSpec(memory_space=pltpu.SMEM), pl.BlockSpec(memory_space=pltpu.VMEM)
    result = jax.ShapeDtypeStruct((layers + 2, 3, rows, width), jnp.float32)
    scratch = lambda *shape: pltpu.VMEM(shape, jnp.float32)
    own, outside = pl.pallas_call(
        lambda *refs: kernel(blocks, groups, *refs),
        out_shape=(result, result),
        in_specs=[smem, smem] + [vmem] * 4,
        out_specs=(vmem, vmem),
        scratch_shapes=[
            scratch(layers + 4, 3, tall, width),
            scratch(layers + 4, 3, tall, width),
            scratch(2, layers + 4, 3, tall, width),
            scratch(2, layers + 4, 3, tall, width),
            scratch(3, 3, layers + 2, tall, width),
            scratch(layers + 2, 3, rows, width),
            scratch(layers + 2, rows, width),
            scratch(3, layers, tall, width),
            scratch(3, layers + 2, 3, rows, width),
        ],
        compiler_params=pltpu.CompilerParams(vmem_limit_bytes=56 * 1024 * 1024),
        cost_estimate=pl.CostEstimate(flops=500 * 4 * layers * rows * width, bytes_accessed=8 << 20, transcendentals=0),
        name="smooth",
    )(weights, inverse, m.reshape(layers + 4, 3, rows, width), mh.reshape(layers + 4, 3, rows, width), c, ch.reshape(c.shape))

    to_right = shift(outside[..., 0], "grp", 1)
    to_left = shift(outside[..., width - 1], "grp", -1)
    column = jnp.arange(width)
    own = own + jnp.where(column == 0, to_right[..., None], 0.0) + jnp.where(column == width - 1, to_left[..., None], 0.0)
    from_low = shift(own[layers + 1, 1:], "blk", 1)
    from_high = shift(own[0, 1:], "blk", -1)
    total = own[1 : layers + 1]
    total = total.at[0, 1:].add(from_low).at[layers - 1, 1:].add(from_high)
    return jnp.swapaxes(total, 0, 1) * mask_float


def solution(mesh):
    return jax.shard_map(
        local,
        mesh=mesh,
        in_specs=(
            P(None, "blk", None, "grp"),
            P(None, "blk", None, "grp"),
            P("grp", "blk", None, None),
            P(),
        ),
        out_specs=P(None, "blk", None, "grp"),
        check_vma=False,
    )
```

```python
import jax
import jax.numpy as jnp
from jax import lax
from jax.experimental import pallas as pl
from jax.experimental.pallas import tpu as pltpu
from jax.sharding import PartitionSpec as P

OMEGA = 0.8
PAD = 8


def place_of(shift_x, shift_y, shift_z):
    return 9 * (shift_x + 1) + 3 * (shift_y + 1) + (shift_z + 1)


def blank_tables():
    return [
        [[[0.0, 0.0, 0.0] for row_one in range(3)] for place in range(27)] for space in range(4)
    ]


def restriction_tables():
    forward = blank_tables()
    centre = place_of(0, 0, 0)
    for comp in range(3):
        forward[0][centre][comp][comp] = 1.0
        others = [axis_one for axis_one in range(3) if axis_one != comp]
        for first_off in (0, -1):
            for second_off in (0, -1):
                vector = [0, 0, 0]
                vector[others[0]] = first_off
                vector[others[1]] = second_off
                forward[1][place_of(*vector)][comp][comp] += 0.25
        along_p = (comp + 1) % 3
        along_q = (comp + 2) % 3
        forward[2][centre][comp][along_q] += 1.0
        forward[2][centre][comp][along_p] -= 1.0
        vector = [0, 0, 0]
        vector[along_p] = -1
        forward[2][place_of(*vector)][comp][along_q] -= 1.0
        vector = [0, 0, 0]
        vector[along_q] = -1
        forward[2][place_of(*vector)][comp][along_p] += 1.0
    for comp in range(3):
        for shift_x in (-1, 0, 1):
            for shift_y in (-1, 0, 1):
                for shift_z in (-1, 0, 1):
                    source = list(forward[2][place_of(shift_x, shift_y, shift_z)][comp])
                    if abs(source[0]) + abs(source[1]) + abs(source[2]) == 0:
                        continue
                    vector = [shift_x, shift_y, shift_z]
                    vector[comp] += 1
                    for column in range(3):
                        forward[3][place_of(shift_x, shift_y, shift_z)][comp][column] += (
                            0.5 * source[column]
                        )
                        forward[3][place_of(*vector)][comp][column] += 0.5 * source[column]
    backward = blank_tables()
    for space in range(4):
        for shift_x in (-1, 0, 1):
            for shift_y in (-1, 0, 1):
                for shift_z in (-1, 0, 1):
                    for row_one in range(3):
                        for column in range(3):
                            backward[space][place_of(-shift_x, -shift_y, -shift_z)][row_one][
                                column
                            ] = forward[space][place_of(shift_x, shift_y, shift_z)][column][row_one]
    return (forward, backward)


MESH = pl.DeviceIdType.MESH


def terms_of(table):
    rows = [[] for comp in range(3)]
    for dx in (-1, 0, 1):
        for dy in (-1, 0, 1):
            for dz in (-1, 0, 1):
                for row in range(3):
                    for column in range(3):
                        weight = table[place_of(dx, dy, dz)][row][column]
                        if weight != 0.0:
                            rows[row].append((dx, dy, dz, column, weight))
    return rows


def weighted(terms, load):
    groups = {}
    for dx, dy, dz, column, weight in terms:
        piece = load(dx, dy, dz, column)
        held = groups.get(abs(weight))
        if held is None:
            groups[abs(weight)] = piece if weight > 0 else -piece
        else:
            groups[abs(weight)] = held + piece if weight > 0 else held - piece
    total = None
    for size, held in groups.items():
        held = held if size == 1.0 else held * size
        total = held if total is None else total + held
    return total


def ring(own, beside, step, lane):
    width = own.shape[-1]
    turn = 1 if step < 0 else width - 1
    edge = 0 if step < 0 else width - 1
    own_turned = pltpu.roll(own, turn, own.ndim - 1)
    beside_turned = pltpu.roll(beside, turn, own.ndim - 1)
    at_edge = lane == edge
    return (
        jnp.where(at_edge, beside_turned, own_turned),
        jnp.where(at_edge, own_turned, beside_turned),
    )


def first_stage(space, spots, forward, inverse, m, mh, c, ch, mz, mhz, f, rs, edges, layers, tall):
    first_block, last_block, first_lanes, last_lanes = edges
    rows, chunk, width = tall - 2 * PAD, 16, m.shape[-1]
    lane = lax.broadcasted_iota(jnp.int32, (chunk, width), 1)
    table = terms_of(forward[space])
    start, step, number = spots

    @pl.loop(0, number)
    def _(turn):
        layer = start + turn * step
        off = jnp.logical_or(
            jnp.logical_and(first_block, layer == 0),
            jnp.logical_and(last_block, layer == layers + 1),
        )
        off_left = jnp.logical_or(off, first_lanes).astype(jnp.int32)
        off_right = jnp.logical_or(off, last_lanes).astype(jnp.int32)

        @pl.loop(0, rows // chunk)
        def _(i):
            def at(shift=0):
                return pl.ds(i * chunk + (PAD + shift), chunk)

            flat = pl.ds(i * chunk, chunk)
            scale = OMEGA / c[space, layer, flat, :]
            scale_h = OMEGA / ch[space, layer, flat, :]
            for comp in range(3):
                def own(dx, dy, dz, column):
                    place = m if dz == 0 else mz.at[(dz + 1) // 2]
                    return place[layer + 1 + dx, column, at(dy), :]

                def beside(dx, dy, dz, column):
                    place = mh if dz == 0 else mhz.at[(dz + 1) // 2]
                    return place[layer + 1 + dx, column, at(dy), :]

                centre = inverse[space * 3 + comp]
                restricted = weighted(table[comp], own)
                rs[space, layer, comp, flat, :] = restricted
                value = jnp.where(off, 0.0, restricted * (scale * centre))
                value_h = weighted(table[comp], beside) * (scale_h * centre)
                gone = jnp.where(lane == 0, off_right, off_left)
                value_h = jnp.where(gone != 0, 0.0, value_h)
                f[space, 1, comp, layer, at(), :] = value
                f[space, 0, comp, layer, at(), :] = ring(value, value_h, -1, lane)[0]
                f[space, 2, comp, layer, at(), :] = ring(value, value_h, 1, lane)[0]


def second_stage(space, backward, weights, inverse, c, f, rs, sec, b, layers, tall):
    rows, chunk, width = tall - 2 * PAD, 16, c.shape[-1]
    base = space * 243

    @pl.loop(0, rows // chunk)
    def _(i):
        def at(shift=0):
            return pl.ds(i * chunk + (PAD + shift), chunk)

        flat = pl.ds(i * chunk, chunk)
        total = [[None] * 3 for layer in range(layers)]
        for dy in (-1, 0, 1):
            for dz in (-1, 0, 1):
                for column in range(3):
                    planes = [f[space, dz + 1, column, layer, at(dy), :] for layer in range(layers + 2)]
                    for dx in (-1, 0, 1):
                        for comp in range(3):
                            weight = weights[base + place_of(dx, dy, dz) * 9 + comp * 3 + column]
                            for layer in range(layers):
                                piece = planes[layer + 1 + dx] * weight
                                held = total[layer][comp]
                                total[layer][comp] = piece if held is None else held + piece
        for layer in range(layers):
            coeff = c[space, layer + 1, flat, :]
            scale = OMEGA / coeff
            for comp in range(3):
                left = rs[space, layer + 1, comp, flat, :] - coeff * total[layer][comp]
                value = f[space, 1, comp, layer + 1, at(), :]
                sec[comp, layer, at(), :] = value + left * (scale * inverse[space * 3 + comp])

    table = terms_of(backward[space])

    @pl.loop(0, rows // chunk)
    def _(i):
        def at(shift=0):
            return pl.ds(i * chunk + (PAD + shift), chunk)

        flat = pl.ds(i * chunk, chunk)
        for layer in range(layers + 2):
            for comp in range(3):
                for dz in (-1, 0, 1):
                    terms = [
                        term
                        for term in table[comp]
                        if term[2] == dz and 0 <= layer - 1 + term[0] < layers
                    ]
                    if terms:
                        def load(dx, dy, dz, column):
                            return sec[column, layer - 1 + dx, at(dy), :]

                        value = weighted(terms, load)
                        if space > 0:
                            value = value + b[dz + 1, layer, comp, flat, :]
                        b[dz + 1, layer, comp, flat, :] = value
                    elif space == 0:
                        b[dz + 1, layer, comp, flat, :] = jnp.zeros((chunk, width), jnp.float32)


def kernel(
    weights, inverse, residual, mask, cond, out,
    m, mh, mz, mhz, c, ch, f, rs, sec, b,
    m_out, m_got, c_out, c_got, turned, sums, x_got, l_out, l_got,
    send_m, got_m, send_s, got_s, send_c, got_c, send_t, got_t, send_x, got_x, send_l, got_l,
):
    groups, blocks = lax.axis_size("grp"), lax.axis_size("blk")
    group, block = lax.axis_index("grp"), lax.axis_index("blk")
    layers, tall, width = m.shape[0] - 4, m.shape[2], m.shape[3]
    rows, chunk = tall - 2 * PAD, 16
    body = pl.ds(PAD, rows)
    lane = lax.broadcasted_iota(jnp.int32, (chunk, width), 1)
    edges = (block == 0, block == blocks - 1, group == 0, group == groups - 1)
    forward, backward = restriction_tables()

    def there(db):
        return jnp.logical_and(block + db >= 0, block + db < blocks)

    def beside(dg):
        return jnp.logical_and(group + dg >= 0, group + dg < groups)

    zeros = jnp.zeros((PAD, width), jnp.float32)
    plane_zeros = jnp.zeros((rows, width), jnp.float32)
    for layer in (0, 1, layers + 2, layers + 3):
        for comp in range(3):
            m[layer, comp, body, :] = plane_zeros
    m_got[...] = jnp.zeros_like(m_got)
    c_got[...] = jnp.ones_like(c_got)
    l_got[...] = jnp.zeros_like(l_got)
    x_got[...] = jnp.zeros_like(x_got)
    c[:, 0] = jnp.ones((4, rows, width), jnp.float32)
    c[:, layers + 1] = jnp.ones((4, rows, width), jnp.float32)

    barrier = pltpu.get_barrier_semaphore()
    for db in (-1, 0, 1):
        for turn in range(groups):
            if db == 0 and turn == 0:
                continue

            @pl.when(there(db))
            def _():
                pl.semaphore_signal(
                    barrier,
                    inc=1,
                    device_id=(lax.rem(group + turn, groups), block + db),
                    device_id_type=MESH,
                )

    for layer in range(layers):
        for comp in range(3):
            value = residual[comp, layer] * mask[comp, layer].astype(jnp.float32)
            m[layer + 2, comp, body, :] = value
            flipped = value.T
            m_out[0, layer, pl.ds(2 * comp, 2), :] = flipped[width - 2 :]
            m_out[1, layer, pl.ds(2 * comp, 2), :] = flipped[:2]
    c_out[...] = jnp.ones_like(c_out)
    for layer in range(layers):
        for part in range(groups):
            flipped = cond[0, layer, :, pl.ds(part * width, width)].T
            if part + 1 < groups:
                c_out[part + 1, pl.ds(2 * layer, 1), :] = flipped[width - 1 :]
            if part > 0:
                c_out[part - 1, pl.ds(2 * layer + 1, 1), :] = flipped[:1]

    neighbours = jnp.where(block > 0, groups, 0) + jnp.where(block < blocks - 1, groups, 0) + groups - 1
    pl.semaphore_wait(barrier, neighbours)

    def remote(src, dst, send, got, dg, db):
        return pltpu.make_async_remote_copy(
            src_ref=src,
            dst_ref=dst,
            send_sem=send,
            recv_sem=got,
            device_id=(lax.rem(group + dg + groups, groups), block + db),
            device_id_type=MESH,
        )

    two = pl.ds(1, 2)
    masked_copies = []
    for side, db in enumerate((1, -1)):
        near, far = (layers + 1, layers) if db > 0 else (2, 3)
        near_to, far_to = (1, 0) if db > 0 else (layers + 2, layers + 3)
        masked_copies.append((db, 0, remote(m.at[near, :, body], m.at[near_to, :, body], send_m.at[side, 0], got_m.at[side, 0], 0, db)))
        masked_copies.append((db, 0, remote(m.at[far, two, body], m.at[far_to, two, body], send_m.at[side, 1], got_m.at[side, 1], 0, db)))
    for place, db in enumerate((1, 0, -1)):
        for side, dg in enumerate((1, -1)):
            masked_copies.append((db, dg, remote(m_out.at[side], m_got.at[side, pl.ds(place * layers, layers)], send_s.at[place, side], got_s.at[place, side], dg, db)))
    near_copies, far_copies = [], []
    for place, db in enumerate((1, 0, -1)):
        for turn in range(groups):
            if db == 0 and turn == 0:
                continue
            target = lax.rem(group + turn, groups)
            part = pl.ds(pl.multiple_of(target * width, width), width)
            if db == 0:
                src, dst = cond.at[0, :, :, part], c.at[group, pl.ds(1, layers)]
            elif db > 0:
                src, dst = cond.at[0, pl.ds(layers - 1, 1), :, part], c.at[group, pl.ds(0, 1)]
            else:
                src, dst = cond.at[0, pl.ds(0, 1), :, part], c.at[group, pl.ds(layers + 1, 1)]
            held = near_copies if db == 0 else far_copies
            held.append((db, 0, remote(c_out.at[target], c_got.at[place, group], send_t.at[place, turn], got_t.at[place, turn], turn, db)))
            held.append((db, 0, remote(src, dst, send_c.at[place, turn], got_c.at[place, turn], turn, db)))

    def guarded(db, dg, act):
        if db == 0 and dg == 0:
            act()
        else:
            pl.when(jnp.logical_and(there(db), beside(dg)))(act)

    def start(copies):
        for db, dg, copy in copies:
            guarded(db, dg, copy.start)

    def arrive(copies):
        for db, dg, copy in copies:
            guarded(-db, -dg, copy.wait_recv)

    def sent(copies):
        for db, dg, copy in copies:
            guarded(db, dg, copy.wait_send)

    start(masked_copies)
    start(near_copies)
    start(far_copies)

    own_part = pl.ds(pl.multiple_of(group * width, width), width)
    c[group, pl.ds(1, layers)] = cond[0, :, :, own_part]
    c_got[1, group] = c_out[group]
    for side in (0, 1):
        edge = pl.ds(side * (rows + PAD), PAD)
        for layer in range(layers + 4):
            for comp in range(3):
                m[layer, comp, edge, :] = zeros
                mh[layer, comp, edge, :] = zeros
                for dz in (0, 1):
                    mz[dz, layer, comp, edge, :] = zeros
                    mhz[dz, layer, comp, edge, :] = zeros
        for comp in range(3):
            for layer in range(layers + 2):
                for dz in range(3):
                    for space in range(4):
                        f[space, dz, comp, layer, edge, :] = zeros
            for layer in range(layers):
                sec[comp, layer, edge, :] = zeros

    arrive(masked_copies)
    span = (layers + 4) * 8
    tail = jnp.zeros((width - 2 * span, rows), jnp.float32)
    turned[...] = jnp.concatenate([m_got[0].reshape(span, rows), m_got[1].reshape(span, rows), tail]).T

    @pl.loop(0, (layers + 4) * 3)
    def _(plane):
        layer, comp = plane // 3, plane % 3
        spot = layer * 8 + comp * 2

        @pl.loop(0, rows // chunk)
        def _(i):
            at = pl.ds(i * chunk + PAD, chunk)
            strips = turned[pl.ds(i * chunk, chunk), :]
            before = pltpu.roll(strips, width - 2 - spot, 1)
            after = pltpu.roll(strips, width - span - spot, 1)
            outer = jnp.where(lane < 2, after, jnp.where(lane >= width - 2, before, 0.0))
            own = m[layer, comp, at, :]
            mh[layer, comp, at, :] = outer
            for dz in (0, 1):
                one, other = ring(own, outer, 2 * dz - 1, lane)
                mz[dz, layer, comp, at, :] = one
                mhz[dz, layer, comp, at, :] = other

    def place_lanes(places, spots):
        held = 4 * 8
        tail = jnp.ones((width - held * len(places), rows), jnp.float32)
        turned[...] = jnp.concatenate([c_got[place].reshape(held, rows) for place in places] + [tail]).T
        for space in range(4):
            for spot in spots:
                row = space * 8 + (2 * layers - 2 if spot == 0 else held if spot == layers + 1 else 2 * (spot - 1))

                @pl.loop(0, rows // chunk)
                def _(i):
                    flat = pl.ds(i * chunk, chunk)
                    strips = turned[flat, :]
                    before = pltpu.roll(strips, (2 * width - 1 - row) % width, 1)
                    after = pltpu.roll(strips, (2 * width - 1 - row) % width, 1)
                    ch[space, spot, flat, :] = jnp.where(lane == 0, after, jnp.where(lane == width - 1, before, 1.0))

    arrive(near_copies)
    place_lanes((1,), range(1, layers + 1))
    for space in range(4):
        first_stage(space, (1, 1, layers), forward, inverse, m, mh, c, ch, mz, mhz, f, rs, edges, layers, tall)
    arrive(far_copies)
    place_lanes((0, 2), (0, layers + 1))
    for space in range(4):
        first_stage(space, (0, layers + 1, 2), forward, inverse, m, mh, c, ch, mz, mhz, f, rs, edges, layers, tall)
        second_stage(space, backward, weights, inverse, c, f, rs, sec, b, layers, tall)

    @pl.loop(0, rows // chunk)
    def _(i):
        flat = pl.ds(i * chunk, chunk)
        packed = jnp.zeros((chunk, width), jnp.float32)
        for layer in range(layers + 2):
            for comp in range(3):
                before = pltpu.roll(b[0, layer, comp, flat, :], 1, 1)
                after = pltpu.roll(b[2, layer, comp, flat, :], width - 1, 1)
                own = b[1, layer, comp, flat, :]
                own = own + jnp.where(lane == 0, 0.0, before) + jnp.where(lane == width - 1, 0.0, after)
                sums[layer, comp, flat, :] = own
                spot = comp if layer == 0 else 16 + comp if layer == layers + 1 else 8 + (layer - 1) * 3 + comp
                packed = jnp.where(lane == spot, before[:, :1], packed)
                packed = jnp.where(lane == 24 + spot, after[:, width - 1 :], packed)
        turned[flat, :] = packed
    flipped = turned[...].T
    l_out[...] = flipped[:48].reshape(2, 3, 8, rows)

    last_copies = []
    for side, db in enumerate((1, -1)):
        layer = layers + 1 if db > 0 else 0
        last_copies.append((db, 0, remote(sums.at[layer, two], x_got.at[side], send_x.at[side], got_x.at[side], 0, db)))
    for place, db in enumerate((-1, 0, 1)):
        for side, dg in enumerate((1, -1)):
            last_copies.append((db, dg, remote(l_out.at[side, place], l_got.at[side, place], send_l.at[place, side], got_l.at[place, side], dg, db)))
    start(last_copies)
    sent(masked_copies)
    sent(near_copies)
    sent(far_copies)
    arrive(last_copies)
    tail = jnp.zeros((width - 48, rows), jnp.float32)
    turned[...] = jnp.concatenate([l_got[...].reshape(48, rows), tail]).T

    @pl.loop(0, rows // chunk)
    def _(i):
        flat = pl.ds(i * chunk, chunk)
        strips = turned[flat, :]
        for layer in range(layers):
            for comp in range(3):
                total = sums[layer + 1, comp, flat, :]
                if comp > 0 and layer == 0:
                    total = total + x_got[0, comp - 1, flat, :]
                if comp > 0 and layer == layers - 1:
                    total = total + x_got[1, comp - 1, flat, :]
                spot = 8 + layer * 3 + comp
                low, high = strips[:, spot : spot + 1], strips[:, 24 + spot : 25 + spot]
                if layer == layers - 1:
                    low, high = low + strips[:, comp : comp + 1], high + strips[:, 24 + comp : 25 + comp]
                if layer == 0:
                    low, high = low + strips[:, 16 + comp : 17 + comp], high + strips[:, 40 + comp : 41 + comp]
                total = total + jnp.where(lane == 0, low, 0.0) + jnp.where(lane == width - 1, high, 0.0)
                out[comp, layer, flat, :] = total * mask[comp, layer, flat, :].astype(jnp.float32)
    sent(last_copies)


def local(residual, face_mask, conductivity, stencil):
    _, layers, rows, width = residual.shape
    groups = lax.axis_size("grp")
    tall = rows + 2 * PAD
    weights = stencil.reshape(-1)
    inverse = (1.0 / jnp.diagonal(stencil[:, 13], axis1=1, axis2=2)).reshape(-1)
    smem, vmem = pl.BlockSpec(memory_space=pltpu.SMEM), pl.BlockSpec(memory_space=pltpu.VMEM)
    scratch = lambda *shape: pltpu.VMEM(shape, jnp.float32)
    sems = lambda *shape: pltpu.SemaphoreType.DMA(shape)
    return pl.pallas_call(
        kernel,
        out_shape=jax.ShapeDtypeStruct(residual.shape, jnp.float32),
        in_specs=[smem, smem, vmem, vmem, vmem],
        out_specs=vmem,
        scratch_shapes=[
            scratch(layers + 4, 3, tall, width),
            scratch(layers + 4, 3, tall, width),
            scratch(2, layers + 4, 3, tall, width),
            scratch(2, layers + 4, 3, tall, width),
            scratch(4, layers + 2, rows, width),
            scratch(4, layers + 2, rows, width),
            scratch(4, 3, 3, layers + 2, tall, width),
            scratch(4, layers + 2, 3, rows, width),
            scratch(3, layers, tall, width),
            scratch(3, layers + 2, 3, rows, width),
            scratch(2, layers, 8, rows),
            scratch(2, layers + 4, 8, rows),
            scratch(groups, 8, rows),
            scratch(3, 4, 8, rows),
            scratch(rows, width),
            scratch(layers + 2, 3, rows, width),
            scratch(2, 2, rows, width),
            scratch(2, 3, 8, rows),
            scratch(2, 3, 8, rows),
            sems(2, 2), sems(2, 2), sems(3, 2), sems(3, 2), sems(3, groups), sems(3, groups),
            sems(3, groups), sems(3, groups), sems(2), sems(2), sems(3, 2), sems(3, 2),
        ],
        compiler_params=pltpu.CompilerParams(
            vmem_limit_bytes=60 * 1024 * 1024, collective_id=0, has_side_effects=True
        ),
        name="correct",
    )(weights, inverse, residual, face_mask, conductivity)


def solution(mesh):
    return jax.shard_map(
        local,
        mesh=mesh,
        in_specs=(
            P(None, "blk", None, "grp"),
            P(None, "blk", None, "grp"),
            P("grp", "blk", None, None),
            P(),
        ),
        out_specs=P(None, "blk", None, "grp"),
        check_vma=False,
    )
```

```python
import jax
import jax.numpy as jnp
from jax import lax
from jax.experimental import pallas as pl
from jax.experimental.pallas import tpu as pltpu
from jax.sharding import PartitionSpec as P

OMEGA = 0.8
PAD = 8


def place_of(shift_x, shift_y, shift_z):
    return 9 * (shift_x + 1) + 3 * (shift_y + 1) + (shift_z + 1)


def blank_tables():
    return [
        [[[0.0, 0.0, 0.0] for row_one in range(3)] for place in range(27)] for space in range(4)
    ]


def restriction_tables():
    forward = blank_tables()
    centre = place_of(0, 0, 0)
    for comp in range(3):
        forward[0][centre][comp][comp] = 1.0
        others = [axis_one for axis_one in range(3) if axis_one != comp]
        for first_off in (0, -1):
            for second_off in (0, -1):
                vector = [0, 0, 0]
                vector[others[0]] = first_off
                vector[others[1]] = second_off
                forward[1][place_of(*vector)][comp][comp] += 0.25
        along_p = (comp + 1) % 3
        along_q = (comp + 2) % 3
        forward[2][centre][comp][along_q] += 1.0
        forward[2][centre][comp][along_p] -= 1.0
        vector = [0, 0, 0]
        vector[along_p] = -1
        forward[2][place_of(*vector)][comp][along_q] -= 1.0
        vector = [0, 0, 0]
        vector[along_q] = -1
        forward[2][place_of(*vector)][comp][along_p] += 1.0
    for comp in range(3):
        for shift_x in (-1, 0, 1):
            for shift_y in (-1, 0, 1):
                for shift_z in (-1, 0, 1):
                    source = list(forward[2][place_of(shift_x, shift_y, shift_z)][comp])
                    if abs(source[0]) + abs(source[1]) + abs(source[2]) == 0:
                        continue
                    vector = [shift_x, shift_y, shift_z]
                    vector[comp] += 1
                    for column in range(3):
                        forward[3][place_of(shift_x, shift_y, shift_z)][comp][column] += (
                            0.5 * source[column]
                        )
                        forward[3][place_of(*vector)][comp][column] += 0.5 * source[column]
    backward = blank_tables()
    for space in range(4):
        for shift_x in (-1, 0, 1):
            for shift_y in (-1, 0, 1):
                for shift_z in (-1, 0, 1):
                    for row_one in range(3):
                        for column in range(3):
                            backward[space][place_of(-shift_x, -shift_y, -shift_z)][row_one][
                                column
                            ] = forward[space][place_of(shift_x, shift_y, shift_z)][column][row_one]
    return (forward, backward)


MESH = pl.DeviceIdType.MESH


def terms_of(table):
    rows = [[] for comp in range(3)]
    for dx in (-1, 0, 1):
        for dy in (-1, 0, 1):
            for dz in (-1, 0, 1):
                for row in range(3):
                    for column in range(3):
                        weight = table[place_of(dx, dy, dz)][row][column]
                        if weight != 0.0:
                            rows[row].append((dx, dy, dz, column, weight))
    return rows


def weighted(terms, load):
    groups = {}
    for dx, dy, dz, column, weight in terms:
        piece = load(dx, dy, dz, column)
        held = groups.get(abs(weight))
        if held is None:
            groups[abs(weight)] = piece if weight > 0 else -piece
        else:
            groups[abs(weight)] = held + piece if weight > 0 else held - piece
    total = None
    for size, held in groups.items():
        held = held if size == 1.0 else held * size
        total = held if total is None else total + held
    return total


def ring(own, beside, step, lane):
    width = own.shape[-1]
    turn = 1 if step < 0 else width - 1
    edge = 0 if step < 0 else width - 1
    own_turned = pltpu.roll(own, turn, own.ndim - 1)
    beside_turned = pltpu.roll(beside, turn, own.ndim - 1)
    at_edge = lane == edge
    return (
        jnp.where(at_edge, beside_turned, own_turned),
        jnp.where(at_edge, own_turned, beside_turned),
    )


def inverse_of(weights, space, comp):
    return 1.0 / weights[space * 243 + place_of(0, 0, 0) * 9 + comp * 4]


def first_stage(space, spots, forward, weights, m, mh, c, ch, mz, mhz, f, rs, edges, layers, tall):
    first_block, last_block, first_lanes, last_lanes = edges
    rows, chunk, width = tall - 2 * PAD, 64, m.shape[-1]
    lane = lax.broadcasted_iota(jnp.int32, (chunk, width), 1)
    table = terms_of(forward[space])
    start, step, number = spots
    inverses = [inverse_of(weights, space, comp) for comp in range(3)]

    @pl.loop(0, number)
    def _(turn):
        layer = start + turn * step
        off = jnp.logical_or(
            jnp.logical_and(first_block, layer == 0),
            jnp.logical_and(last_block, layer == layers + 1),
        )
        off_left = jnp.logical_or(off, first_lanes).astype(jnp.int32)
        off_right = jnp.logical_or(off, last_lanes).astype(jnp.int32)

        @pl.loop(0, rows // chunk)
        def _(i):
            def at(shift=0):
                return pl.ds(i * chunk + (PAD + shift), chunk)

            flat = pl.ds(i * chunk, chunk)
            scale = OMEGA / c[space, layer, flat, :]
            scale_h = OMEGA / ch[space, layer, flat, :]
            for comp in range(3):
                def own(dx, dy, dz, column):
                    place = m if dz == 0 else mz.at[(dz + 1) // 2]
                    return place[layer + 1 + dx, column, at(dy), :]

                def beside(dx, dy, dz, column):
                    place = mh if dz == 0 else mhz.at[(dz + 1) // 2]
                    return place[layer + 1 + dx, column, at(dy), :]

                centre = inverses[comp]
                restricted = weighted(table[comp], own)
                rs[space, layer, comp, flat, :] = restricted
                value = jnp.where(off, 0.0, restricted * (scale * centre))
                value_h = weighted(table[comp], beside) * (scale_h * centre)
                gone = jnp.where(lane == 0, off_right, off_left)
                value_h = jnp.where(gone != 0, 0.0, value_h)
                f[space, 1, comp, layer, at(), :] = value
                f[space, 0, comp, layer, at(), :] = ring(value, value_h, -1, lane)[0]
                f[space, 2, comp, layer, at(), :] = ring(value, value_h, 1, lane)[0]


def dense(space, sources, i, weights, f, total, layers, chunk):
    base = space * 243
    for dy in (-1, 0, 1):
        for dz in (-1, 0, 1):
            for column in range(3):
                for source in sources:
                    plane = f[space, dz + 1, column, source, pl.ds(i * chunk + (PAD + dy), chunk), :]
                    for layer in range(layers):
                        dx = source - layer - 1
                        if abs(dx) > 1:
                            continue
                        for comp in range(3):
                            piece = plane * weights[base + place_of(dx, dy, dz) * 9 + comp * 3 + column]
                            held = total[layer][comp]
                            total[layer][comp] = piece if held is None else held + piece


def near_stage(space, weights, f, part, layers, tall):
    chunk = 16

    @pl.loop(0, (tall - 2 * PAD) // chunk)
    def _(i):
        total = [[None] * 3 for layer in range(layers)]
        dense(space, range(1, layers + 1), i, weights, f, total, layers, chunk)
        for layer in range(layers):
            for comp in range(3):
                part[space, layer, comp, pl.ds(i * chunk, chunk), :] = total[layer][comp]


def second_stage(space, backward, weights, c, f, rs, part, sec, b, layers, tall):
    rows, chunk, width = tall - 2 * PAD, 16, c.shape[-1]
    inverses = [inverse_of(weights, space, comp) for comp in range(3)]

    @pl.loop(0, rows // chunk)
    def _(i):
        def at(shift=0):
            return pl.ds(i * chunk + (PAD + shift), chunk)

        flat = pl.ds(i * chunk, chunk)
        total = [[part[space, layer, comp, flat, :] for comp in range(3)] for layer in range(layers)]
        dense(space, (0, layers + 1), i, weights, f, total, layers, chunk)
        for layer in range(layers):
            coeff = c[space, layer + 1, flat, :]
            scale = OMEGA / coeff
            for comp in range(3):
                left = rs[space, layer + 1, comp, flat, :] - coeff * total[layer][comp]
                value = f[space, 1, comp, layer + 1, at(), :]
                sec[comp, layer, at(), :] = value + left * (scale * inverses[comp])

    table = terms_of(backward[space])

    @pl.loop(0, rows // chunk)
    def _(i):
        def at(shift=0):
            return pl.ds(i * chunk + (PAD + shift), chunk)

        flat = pl.ds(i * chunk, chunk)
        for layer in range(layers + 2):
            for comp in range(3):
                for dz in (-1, 0, 1):
                    terms = [
                        term
                        for term in table[comp]
                        if term[2] == dz and 0 <= layer - 1 + term[0] < layers
                    ]
                    if terms:
                        def load(dx, dy, dz, column):
                            return sec[column, layer - 1 + dx, at(dy), :]

                        value = weighted(terms, load)
                        if space > 0:
                            value = value + b[dz + 1, layer, comp, flat, :]
                        b[dz + 1, layer, comp, flat, :] = value
                    elif space == 0:
                        b[dz + 1, layer, comp, flat, :] = jnp.zeros((chunk, width), jnp.float32)


def kernel(
    weights, residual, mask, cond, out,
    m, mh, mz, mhz, c, ch, f, rs, partial, sec, b,
    m_out, m_got, c_out, c_got, turned, sums, x_got, l_out, l_got,
    send_m, got_m, send_s, got_s, send_c, got_c, send_t, got_t, send_x, got_x, send_l, got_l,
):
    groups, blocks = lax.axis_size("grp"), lax.axis_size("blk")
    group, block = lax.axis_index("grp"), lax.axis_index("blk")
    layers, tall, width = m.shape[0] - 4, m.shape[2], m.shape[3]
    rows, chunk = tall - 2 * PAD, 16
    body = pl.ds(PAD, rows)
    lane = lax.broadcasted_iota(jnp.int32, (chunk, width), 1)
    edges = (block == 0, block == blocks - 1, group == 0, group == groups - 1)
    forward, backward = restriction_tables()

    def there(db):
        return jnp.logical_and(block + db >= 0, block + db < blocks)

    def beside(dg):
        return jnp.logical_and(group + dg >= 0, group + dg < groups)

    zeros = jnp.zeros((PAD, width), jnp.float32)
    plane_zeros = jnp.zeros((rows, width), jnp.float32)
    for layer in (0, 1, layers + 2, layers + 3):
        for comp in range(3):
            m[layer, comp, body, :] = plane_zeros
    m_got[...] = jnp.zeros_like(m_got)
    c_got[...] = jnp.ones_like(c_got)
    l_got[...] = jnp.zeros_like(l_got)
    x_got[...] = jnp.zeros_like(x_got)
    c[:, 0] = jnp.ones((4, rows, width), jnp.float32)
    c[:, layers + 1] = jnp.ones((4, rows, width), jnp.float32)

    barrier = pltpu.get_barrier_semaphore()
    for db in (-1, 0, 1):
        for turn in range(groups):
            if db == 0 and turn == 0:
                continue

            @pl.when(there(db))
            def _():
                pl.semaphore_signal(
                    barrier,
                    inc=1,
                    device_id=(lax.rem(group + turn, groups), block + db),
                    device_id_type=MESH,
                )

    for layer in range(layers):
        for comp in range(3):
            value = residual[comp, layer] * mask[comp, layer].astype(jnp.float32)
            m[layer + 2, comp, body, :] = value
            flipped = value.T
            m_out[0, layer, pl.ds(2 * comp, 2), :] = flipped[width - 2 :]
            m_out[1, layer, pl.ds(2 * comp, 2), :] = flipped[:2]
    c_out[...] = jnp.ones_like(c_out)
    for layer in range(layers):
        for part in range(groups):
            flipped = cond[0, layer, :, pl.ds(part * width, width)].T
            if part + 1 < groups:
                c_out[part + 1, pl.ds(2 * layer, 1), :] = flipped[width - 1 :]
            if part > 0:
                c_out[part - 1, pl.ds(2 * layer + 1, 1), :] = flipped[:1]

    neighbours = jnp.where(block > 0, groups, 0) + jnp.where(block < blocks - 1, groups, 0) + groups - 1
    pl.semaphore_wait(barrier, neighbours)

    def remote(src, dst, send, got, dg, db):
        return pltpu.make_async_remote_copy(
            src_ref=src,
            dst_ref=dst,
            send_sem=send,
            recv_sem=got,
            device_id=(lax.rem(group + dg + groups, groups), block + db),
            device_id_type=MESH,
        )

    two = pl.ds(1, 2)
    masked_copies = []
    for side, db in enumerate((1, -1)):
        near, far = (layers + 1, layers) if db > 0 else (2, 3)
        near_to, far_to = (1, 0) if db > 0 else (layers + 2, layers + 3)
        masked_copies.append((db, 0, remote(m.at[near, :, body], m.at[near_to, :, body], send_m.at[side, 0], got_m.at[side, 0], 0, db)))
        masked_copies.append((db, 0, remote(m.at[far, two, body], m.at[far_to, two, body], send_m.at[side, 1], got_m.at[side, 1], 0, db)))
    for place, db in enumerate((1, 0, -1)):
        for side, dg in enumerate((1, -1)):
            masked_copies.append((db, dg, remote(m_out.at[side], m_got.at[side, pl.ds(place * layers, layers)], send_s.at[place, side], got_s.at[place, side], dg, db)))
    near_copies, far_copies = [], []
    for place, db in enumerate((1, 0, -1)):
        for turn in range(groups):
            if db == 0 and turn == 0:
                continue
            target = lax.rem(group + turn, groups)
            part = pl.ds(pl.multiple_of(target * width, width), width)
            if db == 0:
                src, dst = cond.at[0, :, :, part], c.at[group, pl.ds(1, layers)]
            elif db > 0:
                src, dst = cond.at[0, pl.ds(layers - 1, 1), :, part], c.at[group, pl.ds(0, 1)]
            else:
                src, dst = cond.at[0, pl.ds(0, 1), :, part], c.at[group, pl.ds(layers + 1, 1)]
            held = near_copies if db == 0 else far_copies
            held.append((db, 0, remote(c_out.at[target], c_got.at[place, group], send_t.at[place, turn], got_t.at[place, turn], turn, db)))
            held.append((db, 0, remote(src, dst, send_c.at[place, turn], got_c.at[place, turn], turn, db)))

    def guarded(db, dg, act):
        if db == 0 and dg == 0:
            act()
        else:
            pl.when(jnp.logical_and(there(db), beside(dg)))(act)

    def start(copies):
        for db, dg, copy in copies:
            guarded(db, dg, copy.start)

    def arrive(copies):
        for db, dg, copy in copies:
            guarded(-db, -dg, copy.wait_recv)

    def sent(copies):
        for db, dg, copy in copies:
            guarded(db, dg, copy.wait_send)

    start(masked_copies)
    start(near_copies)
    start(far_copies)

    own_part = pl.ds(pl.multiple_of(group * width, width), width)
    c[group, pl.ds(1, layers)] = cond[0, :, :, own_part]
    c_got[1, group] = c_out[group]
    for side in (0, 1):
        edge = pl.ds(side * (rows + PAD), PAD)
        for layer in range(layers + 4):
            for comp in range(3):
                m[layer, comp, edge, :] = zeros
                mh[layer, comp, edge, :] = zeros
                for dz in (0, 1):
                    mz[dz, layer, comp, edge, :] = zeros
                    mhz[dz, layer, comp, edge, :] = zeros
        for comp in range(3):
            for layer in range(layers + 2):
                for dz in range(3):
                    for space in range(4):
                        f[space, dz, comp, layer, edge, :] = zeros
            for layer in range(layers):
                sec[comp, layer, edge, :] = zeros

    arrive(masked_copies)
    span = (layers + 4) * 8
    tail = jnp.zeros((width - 2 * span, rows), jnp.float32)
    turned[...] = jnp.concatenate([m_got[0].reshape(span, rows), m_got[1].reshape(span, rows), tail]).T

    tall_lane = lax.broadcasted_iota(jnp.int32, (rows, width), 1)

    @pl.loop(0, (layers + 4) * 3)
    def _(plane):
        layer, comp = plane // 3, plane % 3
        spot = layer * 8 + comp * 2
        strips = turned[...]
        before = pltpu.roll(strips, width - 2 - spot, 1)
        after = pltpu.roll(strips, width - span - spot, 1)
        outer = jnp.where(tall_lane < 2, after, jnp.where(tall_lane >= width - 2, before, 0.0))
        own = m[layer, comp, body, :]
        mh[layer, comp, body, :] = outer
        for dz in (0, 1):
            one, other = ring(own, outer, 2 * dz - 1, tall_lane)
            mz[dz, layer, comp, body, :] = one
            mhz[dz, layer, comp, body, :] = other

    def place_lanes(places, spots):
        held = 4 * 8
        tail = jnp.ones((width - held * len(places), rows), jnp.float32)
        turned[...] = jnp.concatenate([c_got[place].reshape(held, rows) for place in places] + [tail]).T
        for space in range(4):
            for spot in spots:
                row = space * 8 + (2 * layers - 2 if spot == 0 else held if spot == layers + 1 else 2 * (spot - 1))
                strips = pltpu.roll(turned[...], (2 * width - 1 - row) % width, 1)
                outermost = jnp.logical_or(tall_lane == 0, tall_lane == width - 1)
                ch[space, spot] = jnp.where(outermost, strips, 1.0)

    arrive(near_copies)
    place_lanes((1,), range(1, layers + 1))
    for space in range(4):
        first_stage(space, (1, 1, layers), forward, weights, m, mh, c, ch, mz, mhz, f, rs, edges, layers, tall)
        near_stage(space, weights, f, partial, layers, tall)
    arrive(far_copies)
    place_lanes((0, 2), (0, layers + 1))
    for space in range(4):
        first_stage(space, (0, layers + 1, 2), forward, weights, m, mh, c, ch, mz, mhz, f, rs, edges, layers, tall)
        second_stage(space, backward, weights, c, f, rs, partial, sec, b, layers, tall)

    @pl.loop(0, rows // chunk)
    def _(i):
        flat = pl.ds(i * chunk, chunk)
        packed = jnp.zeros((chunk, width), jnp.float32)
        for layer in range(layers + 2):
            for comp in range(3):
                before = pltpu.roll(b[0, layer, comp, flat, :], 1, 1)
                after = pltpu.roll(b[2, layer, comp, flat, :], width - 1, 1)
                own = b[1, layer, comp, flat, :]
                own = own + jnp.where(lane == 0, 0.0, before) + jnp.where(lane == width - 1, 0.0, after)
                sums[layer, comp, flat, :] = own
                spot = comp if layer == 0 else 16 + comp if layer == layers + 1 else 8 + (layer - 1) * 3 + comp
                packed = jnp.where(lane == spot, before[:, :1], packed)
                packed = jnp.where(lane == 24 + spot, after[:, width - 1 :], packed)
        turned[flat, :] = packed
    flipped = turned[...].T
    l_out[...] = flipped[:48].reshape(2, 3, 8, rows)

    last_copies = []
    for side, db in enumerate((1, -1)):
        layer = layers + 1 if db > 0 else 0
        last_copies.append((db, 0, remote(sums.at[layer, two], x_got.at[side], send_x.at[side], got_x.at[side], 0, db)))
    for place, db in enumerate((-1, 0, 1)):
        for side, dg in enumerate((1, -1)):
            last_copies.append((db, dg, remote(l_out.at[side, place], l_got.at[side, place], send_l.at[place, side], got_l.at[place, side], dg, db)))
    start(last_copies)
    sent(masked_copies)
    sent(near_copies)
    sent(far_copies)
    arrive(last_copies)
    tail = jnp.zeros((width - 48, rows), jnp.float32)
    turned[...] = jnp.concatenate([l_got[...].reshape(48, rows), tail]).T

    @pl.loop(0, rows // chunk)
    def _(i):
        flat = pl.ds(i * chunk, chunk)
        strips = turned[flat, :]
        for layer in range(layers):
            for comp in range(3):
                total = sums[layer + 1, comp, flat, :]
                if comp > 0 and layer == 0:
                    total = total + x_got[0, comp - 1, flat, :]
                if comp > 0 and layer == layers - 1:
                    total = total + x_got[1, comp - 1, flat, :]
                spot = 8 + layer * 3 + comp
                low, high = strips[:, spot : spot + 1], strips[:, 24 + spot : 25 + spot]
                if layer == layers - 1:
                    low, high = low + strips[:, comp : comp + 1], high + strips[:, 24 + comp : 25 + comp]
                if layer == 0:
                    low, high = low + strips[:, 16 + comp : 17 + comp], high + strips[:, 40 + comp : 41 + comp]
                total = total + jnp.where(lane == 0, low, 0.0) + jnp.where(lane == width - 1, high, 0.0)
                out[comp, layer, flat, :] = total * mask[comp, layer, flat, :].astype(jnp.float32)
    sent(last_copies)


def local(residual, face_mask, conductivity, stencil):
    _, layers, rows, width = residual.shape
    groups = lax.axis_size("grp")
    tall = rows + 2 * PAD
    weights = stencil.reshape(-1)
    smem, vmem = pl.BlockSpec(memory_space=pltpu.SMEM), pl.BlockSpec(memory_space=pltpu.VMEM)
    scratch = lambda *shape: pltpu.VMEM(shape, jnp.float32)
    sems = lambda *shape: pltpu.SemaphoreType.DMA(shape)
    return pl.pallas_call(
        kernel,
        out_shape=jax.ShapeDtypeStruct(residual.shape, jnp.float32),
        in_specs=[smem, vmem, vmem, vmem],
        out_specs=vmem,
        scratch_shapes=[
            scratch(layers + 4, 3, tall, width),
            scratch(layers + 4, 3, tall, width),
            scratch(2, layers + 4, 3, tall, width),
            scratch(2, layers + 4, 3, tall, width),
            scratch(4, layers + 2, rows, width),
            scratch(4, layers + 2, rows, width),
            scratch(4, 3, 3, layers + 2, tall, width),
            scratch(4, layers + 2, 3, rows, width),
            scratch(4, layers, 3, rows, width),
            scratch(3, layers, tall, width),
            scratch(3, layers + 2, 3, rows, width),
            scratch(2, layers, 8, rows),
            scratch(2, layers + 4, 8, rows),
            scratch(groups, 8, rows),
            scratch(3, 4, 8, rows),
            scratch(rows, width),
            scratch(layers + 2, 3, rows, width),
            scratch(2, 2, rows, width),
            scratch(2, 3, 8, rows),
            scratch(2, 3, 8, rows),
            sems(2, 2), sems(2, 2), sems(3, 2), sems(3, 2), sems(3, groups), sems(3, groups),
            sems(3, groups), sems(3, groups), sems(2), sems(2), sems(3, 2), sems(3, 2),
        ],
        compiler_params=pltpu.CompilerParams(
            vmem_limit_bytes=60 * 1024 * 1024, collective_id=0, has_side_effects=True
        ),
        name="correct",
    )(weights, residual, face_mask, conductivity)


def solution(mesh):
    return jax.shard_map(
        local,
        mesh=mesh,
        in_specs=(
            P(None, "blk", None, "grp"),
            P(None, "blk", None, "grp"),
            P("grp", "blk", None, None),
            P(),
        ),
        out_specs=P(None, "blk", None, "grp"),
        check_vma=False,
    )
```

```python
import jax
import jax.numpy as jnp
from jax import lax
from jax.experimental import pallas as pl
from jax.experimental.pallas import tpu as pltpu
from jax.sharding import PartitionSpec as P

OMEGA = 0.8
PAD = 8


def place_of(shift_x, shift_y, shift_z):
    return 9 * (shift_x + 1) + 3 * (shift_y + 1) + (shift_z + 1)


def blank_tables():
    return [
        [[[0.0, 0.0, 0.0] for row_one in range(3)] for place in range(27)] for space in range(4)
    ]


def restriction_tables():
    forward = blank_tables()
    centre = place_of(0, 0, 0)
    for comp in range(3):
        forward[0][centre][comp][comp] = 1.0
        others = [axis_one for axis_one in range(3) if axis_one != comp]
        for first_off in (0, -1):
            for second_off in (0, -1):
                vector = [0, 0, 0]
                vector[others[0]] = first_off
                vector[others[1]] = second_off
                forward[1][place_of(*vector)][comp][comp] += 0.25
        along_p = (comp + 1) % 3
        along_q = (comp + 2) % 3
        forward[2][centre][comp][along_q] += 1.0
        forward[2][centre][comp][along_p] -= 1.0
        vector = [0, 0, 0]
        vector[along_p] = -1
        forward[2][place_of(*vector)][comp][along_q] -= 1.0
        vector = [0, 0, 0]
        vector[along_q] = -1
        forward[2][place_of(*vector)][comp][along_p] += 1.0
    for comp in range(3):
        for shift_x in (-1, 0, 1):
            for shift_y in (-1, 0, 1):
                for shift_z in (-1, 0, 1):
                    source = list(forward[2][place_of(shift_x, shift_y, shift_z)][comp])
                    if abs(source[0]) + abs(source[1]) + abs(source[2]) == 0:
                        continue
                    vector = [shift_x, shift_y, shift_z]
                    vector[comp] += 1
                    for column in range(3):
                        forward[3][place_of(shift_x, shift_y, shift_z)][comp][column] += (
                            0.5 * source[column]
                        )
                        forward[3][place_of(*vector)][comp][column] += 0.5 * source[column]
    backward = blank_tables()
    for space in range(4):
        for shift_x in (-1, 0, 1):
            for shift_y in (-1, 0, 1):
                for shift_z in (-1, 0, 1):
                    for row_one in range(3):
                        for column in range(3):
                            backward[space][place_of(-shift_x, -shift_y, -shift_z)][row_one][
                                column
                            ] = forward[space][place_of(shift_x, shift_y, shift_z)][column][row_one]
    return (forward, backward)


MESH = pl.DeviceIdType.MESH


def terms_of(table):
    rows = [[] for comp in range(3)]
    for dx in (-1, 0, 1):
        for dy in (-1, 0, 1):
            for dz in (-1, 0, 1):
                for row in range(3):
                    for column in range(3):
                        weight = table[place_of(dx, dy, dz)][row][column]
                        if weight != 0.0:
                            rows[row].append((dx, dy, dz, column, weight))
    return rows


def weighted(terms, load):
    groups = {}
    for dx, dy, dz, column, weight in terms:
        piece = load(dx, dy, dz, column)
        held = groups.get(abs(weight))
        if held is None:
            groups[abs(weight)] = piece if weight > 0 else -piece
        else:
            groups[abs(weight)] = held + piece if weight > 0 else held - piece
    total = None
    for size, held in groups.items():
        held = held if size == 1.0 else held * size
        total = held if total is None else total + held
    return total


def ring(own, beside, step, lane):
    width = own.shape[-1]
    turn = 1 if step < 0 else width - 1
    edge = 0 if step < 0 else width - 1
    own_turned = pltpu.roll(own, turn, own.ndim - 1)
    beside_turned = pltpu.roll(beside, turn, own.ndim - 1)
    at_edge = lane == edge
    return (
        jnp.where(at_edge, beside_turned, own_turned),
        jnp.where(at_edge, own_turned, beside_turned),
    )


def inverse_of(weights, space, comp):
    return 1.0 / weights[space * 243 + place_of(0, 0, 0) * 9 + comp * 4]


def first_stage(space, spots, forward, weights, m, mh, c, ch, mz, mhz, f, rs, edges, layers, tall):
    first_block, last_block, first_lanes, last_lanes = edges
    rows, chunk, width = tall - 2 * PAD, 64, m.shape[-1]
    lane = lax.broadcasted_iota(jnp.int32, (chunk, width), 1)
    table = terms_of(forward[space])
    start, step, number = spots
    inverses = [inverse_of(weights, space, comp) for comp in range(3)]

    @pl.loop(0, number)
    def _(turn):
        layer = start + turn * step
        off = jnp.logical_or(
            jnp.logical_and(first_block, layer == 0),
            jnp.logical_and(last_block, layer == layers + 1),
        )
        off_left = jnp.logical_or(off, first_lanes).astype(jnp.int32)
        off_right = jnp.logical_or(off, last_lanes).astype(jnp.int32)

        @pl.loop(0, rows // chunk)
        def _(i):
            def at(shift=0):
                return pl.ds(i * chunk + (PAD + shift), chunk)

            flat = pl.ds(i * chunk, chunk)
            scale = OMEGA / c[space, layer, flat, :]
            scale_h = OMEGA / ch[space, layer, flat, :]
            for comp in range(3):
                def own(dx, dy, dz, column):
                    place = m if dz == 0 else mz.at[(dz + 1) // 2]
                    return place[layer + 1 + dx, column, at(dy), :]

                def beside(dx, dy, dz, column):
                    place = mh if dz == 0 else mhz.at[(dz + 1) // 2]
                    return place[layer + 1 + dx, column, at(dy), :]

                centre = inverses[comp]
                restricted = weighted(table[comp], own)
                rs[space, layer, comp, flat, :] = restricted
                value = jnp.where(off, 0.0, restricted * (scale * centre))
                value_h = weighted(table[comp], beside) * (scale_h * centre)
                gone = jnp.where(lane == 0, off_right, off_left)
                value_h = jnp.where(gone != 0, 0.0, value_h)
                f[space, 1, comp, layer, at(), :] = value
                f[space, 0, comp, layer, at(), :] = ring(value, value_h, -1, lane)[0]
                f[space, 2, comp, layer, at(), :] = ring(value, value_h, 1, lane)[0]


def dense(space, sources, i, weights, f, total, layers, chunk):
    base = space * 243
    for dy in (-1, 0, 1):
        for dz in (-1, 0, 1):
            for column in range(3):
                for source in sources:
                    plane = f[space, dz + 1, column, source, pl.ds(i * chunk + (PAD + dy), chunk), :]
                    for layer in range(layers):
                        dx = source - layer - 1
                        if abs(dx) > 1:
                            continue
                        for comp in range(3):
                            piece = plane * weights[base + place_of(dx, dy, dz) * 9 + comp * 3 + column]
                            held = total[layer][comp]
                            total[layer][comp] = piece if held is None else held + piece


def near_stage(space, sources, fresh, weights, f, part, layers, tall):
    chunk = 16

    @pl.loop(0, (tall - 2 * PAD) // chunk)
    def _(i):
        flat = pl.ds(i * chunk, chunk)
        total = [
            [None if fresh else part[space, layer, comp, flat, :] for comp in range(3)]
            for layer in range(layers)
        ]
        dense(space, sources, i, weights, f, total, layers, chunk)
        for layer in range(layers):
            for comp in range(3):
                part[space, layer, comp, pl.ds(i * chunk, chunk), :] = total[layer][comp]


def second_stage(space, backward, weights, c, f, rs, part, sec, b, layers, tall):
    rows, chunk, width = tall - 2 * PAD, 16, c.shape[-1]
    inverses = [inverse_of(weights, space, comp) for comp in range(3)]

    @pl.loop(0, rows // chunk)
    def _(i):
        def at(shift=0):
            return pl.ds(i * chunk + (PAD + shift), chunk)

        flat = pl.ds(i * chunk, chunk)
        total = [[part[space, layer, comp, flat, :] for comp in range(3)] for layer in range(layers)]
        dense(space, (0, layers + 1), i, weights, f, total, layers, chunk)
        for layer in range(layers):
            coeff = c[space, layer + 1, flat, :]
            scale = OMEGA / coeff
            for comp in range(3):
                left = rs[space, layer + 1, comp, flat, :] - coeff * total[layer][comp]
                value = f[space, 1, comp, layer + 1, at(), :]
                sec[comp, layer, at(), :] = value + left * (scale * inverses[comp])

    table = terms_of(backward[space])

    @pl.loop(0, rows // chunk)
    def _(i):
        def at(shift=0):
            return pl.ds(i * chunk + (PAD + shift), chunk)

        flat = pl.ds(i * chunk, chunk)
        for layer in range(layers + 2):
            for comp in range(3):
                for dz in (-1, 0, 1):
                    terms = [
                        term
                        for term in table[comp]
                        if term[2] == dz and 0 <= layer - 1 + term[0] < layers
                    ]
                    if terms:
                        def load(dx, dy, dz, column):
                            return sec[column, layer - 1 + dx, at(dy), :]

                        value = weighted(terms, load)
                        if space > 0:
                            value = value + b[dz + 1, layer, comp, flat, :]
                        b[dz + 1, layer, comp, flat, :] = value
                    elif space == 0:
                        b[dz + 1, layer, comp, flat, :] = jnp.zeros((chunk, width), jnp.float32)


def kernel(
    weights, residual, mask, cond, out,
    m, mh, mz, mhz, c, ch, f, rs, partial, sec, b,
    m_out, m_got, c_out, c_got, turned, sums, x_got, l_out, l_got,
    send_m, got_m, send_s, got_s, send_c, got_c, send_t, got_t, send_x, got_x, send_l, got_l,
):
    groups, blocks = lax.axis_size("grp"), lax.axis_size("blk")
    group, block = lax.axis_index("grp"), lax.axis_index("blk")
    layers, tall, width = m.shape[0] - 4, m.shape[2], m.shape[3]
    rows, chunk = tall - 2 * PAD, 16
    body = pl.ds(PAD, rows)
    lane = lax.broadcasted_iota(jnp.int32, (chunk, width), 1)
    edges = (block == 0, block == blocks - 1, group == 0, group == groups - 1)
    forward, backward = restriction_tables()

    def there(db):
        return jnp.logical_and(block + db >= 0, block + db < blocks)

    def beside(dg):
        return jnp.logical_and(group + dg >= 0, group + dg < groups)

    zeros = jnp.zeros((PAD, width), jnp.float32)
    plane_zeros = jnp.zeros((rows, width), jnp.float32)
    for layer in (0, 1, layers + 2, layers + 3):
        for comp in range(3):
            m[layer, comp, body, :] = plane_zeros
    m_got[...] = jnp.zeros_like(m_got)
    c_got[...] = jnp.ones_like(c_got)
    l_got[...] = jnp.zeros_like(l_got)
    x_got[...] = jnp.zeros_like(x_got)
    c[:, 0] = jnp.ones((4, rows, width), jnp.float32)
    c[:, layers + 1] = jnp.ones((4, rows, width), jnp.float32)

    barrier = pltpu.get_barrier_semaphore()
    for db in (-1, 0, 1):
        for turn in range(groups):
            if db == 0 and turn == 0:
                continue

            @pl.when(there(db))
            def _():
                pl.semaphore_signal(
                    barrier,
                    inc=1,
                    device_id=(lax.rem(group + turn, groups), block + db),
                    device_id_type=MESH,
                )

    for layer in range(layers):
        for comp in range(3):
            value = residual[comp, layer] * mask[comp, layer].astype(jnp.float32)
            m[layer + 2, comp, body, :] = value
            flipped = value.T
            m_out[0, layer, pl.ds(2 * comp, 2), :] = flipped[width - 2 :]
            m_out[1, layer, pl.ds(2 * comp, 2), :] = flipped[:2]
    c_out[...] = jnp.ones_like(c_out)
    for layer in range(layers):
        for part in range(groups):
            flipped = cond[0, layer, :, pl.ds(part * width, width)].T
            if part + 1 < groups:
                c_out[part + 1, pl.ds(2 * layer, 1), :] = flipped[width - 1 :]
            if part > 0:
                c_out[part - 1, pl.ds(2 * layer + 1, 1), :] = flipped[:1]

    neighbours = jnp.where(block > 0, groups, 0) + jnp.where(block < blocks - 1, groups, 0) + groups - 1
    pl.semaphore_wait(barrier, neighbours)

    def remote(src, dst, send, got, dg, db):
        return pltpu.make_async_remote_copy(
            src_ref=src,
            dst_ref=dst,
            send_sem=send,
            recv_sem=got,
            device_id=(lax.rem(group + dg + groups, groups), block + db),
            device_id_type=MESH,
        )

    two = pl.ds(1, 2)
    masked_copies, lane_copies = [], []
    for side, db in enumerate((1, -1)):
        near, far = (layers + 1, layers) if db > 0 else (2, 3)
        near_to, far_to = (1, 0) if db > 0 else (layers + 2, layers + 3)
        masked_copies.append((db, 0, remote(m.at[near, :, body], m.at[near_to, :, body], send_m.at[side, 0], got_m.at[side, 0], 0, db)))
        masked_copies.append((db, 0, remote(m.at[far, two, body], m.at[far_to, two, body], send_m.at[side, 1], got_m.at[side, 1], 0, db)))
    for place, db in enumerate((1, 0, -1)):
        for side, dg in enumerate((1, -1)):
            held = lane_copies if db == 0 else masked_copies
            held.append((db, dg, remote(m_out.at[side], m_got.at[side, pl.ds(place * layers, layers)], send_s.at[place, side], got_s.at[place, side], dg, db)))
    near_copies, far_copies = [], []
    for place, db in enumerate((1, 0, -1)):
        for turn in range(groups):
            if db == 0 and turn == 0:
                continue
            target = lax.rem(group + turn, groups)
            part = pl.ds(pl.multiple_of(target * width, width), width)
            if db == 0:
                src, dst = cond.at[0, :, :, part], c.at[group, pl.ds(1, layers)]
            elif db > 0:
                src, dst = cond.at[0, pl.ds(layers - 1, 1), :, part], c.at[group, pl.ds(0, 1)]
            else:
                src, dst = cond.at[0, pl.ds(0, 1), :, part], c.at[group, pl.ds(layers + 1, 1)]
            held = near_copies if db == 0 else far_copies
            held.append((db, 0, remote(c_out.at[target], c_got.at[place, group], send_t.at[place, turn], got_t.at[place, turn], turn, db)))
            held.append((db, 0, remote(src, dst, send_c.at[place, turn], got_c.at[place, turn], turn, db)))

    def guarded(db, dg, act):
        if db == 0 and dg == 0:
            act()
        else:
            pl.when(jnp.logical_and(there(db), beside(dg)))(act)

    def start(copies):
        for db, dg, copy in copies:
            guarded(db, dg, copy.start)

    def arrive(copies):
        for db, dg, copy in copies:
            guarded(-db, -dg, copy.wait_recv)

    def sent(copies):
        for db, dg, copy in copies:
            guarded(db, dg, copy.wait_send)

    start(lane_copies)
    start(masked_copies)
    start(near_copies)
    start(far_copies)

    own_part = pl.ds(pl.multiple_of(group * width, width), width)
    c[group, pl.ds(1, layers)] = cond[0, :, :, own_part]
    c_got[1, group] = c_out[group]
    for side in (0, 1):
        edge = pl.ds(side * (rows + PAD), PAD)
        for layer in range(layers + 4):
            for comp in range(3):
                m[layer, comp, edge, :] = zeros
                mh[layer, comp, edge, :] = zeros
                for dz in (0, 1):
                    mz[dz, layer, comp, edge, :] = zeros
                    mhz[dz, layer, comp, edge, :] = zeros
        for comp in range(3):
            for layer in range(layers + 2):
                for dz in range(3):
                    for space in range(4):
                        f[space, dz, comp, layer, edge, :] = zeros
            for layer in range(layers):
                sec[comp, layer, edge, :] = zeros

    span = layers * 8

    tall_lane = lax.broadcasted_iota(jnp.int32, (rows, width), 1)

    def widen(start):
        tail = jnp.zeros((width - 2 * span, rows), jnp.float32)
        strips = [m_got[side, pl.ds(start, layers)].reshape(span, rows) for side in (0, 1)]
        turned[...] = jnp.concatenate(strips + [tail]).T
        pl.loop(0, layers * 3)(lambda plane: widen_plane(start, plane))

    def widen_plane(start, plane):
        layer, comp = start + plane // 3, plane % 3
        spot = (plane // 3) * 8 + comp * 2
        strips = turned[...]
        before = pltpu.roll(strips, width - 2 - spot, 1)
        after = pltpu.roll(strips, width - span - spot, 1)
        outer = jnp.where(tall_lane < 2, after, jnp.where(tall_lane >= width - 2, before, 0.0))
        own = m[layer, comp, body, :]
        mh[layer, comp, body, :] = outer
        for dz in (0, 1):
            one, other = ring(own, outer, 2 * dz - 1, tall_lane)
            mz[dz, layer, comp, body, :] = one
            mhz[dz, layer, comp, body, :] = other

    def place_lanes(places, spots):
        held = 4 * 8
        tail = jnp.ones((width - held * len(places), rows), jnp.float32)
        turned[...] = jnp.concatenate([c_got[place].reshape(held, rows) for place in places] + [tail]).T
        for space in range(4):
            for spot in spots:
                row = space * 8 + (2 * layers - 2 if spot == 0 else held if spot == layers + 1 else 2 * (spot - 1))
                strips = pltpu.roll(turned[...], (2 * width - 1 - row) % width, 1)
                outermost = jnp.logical_or(tall_lane == 0, tall_lane == width - 1)
                ch[space, spot] = jnp.where(outermost, strips, 1.0)

    whole = tuple(range(1, layers + 1))

    def first(space, start, number):
        first_stage(space, (start, 1, number), forward, weights, m, mh, c, ch, mz, mhz, f, rs, edges, layers, tall)

    arrive(lane_copies)
    widen(2)
    arrive(near_copies)
    place_lanes((1,), whole)
    first(0, 1, layers)
    near_stage(0, whole, True, weights, f, partial, layers, tall)
    for space in (1, 2):
        first(space, 2, layers - 1)
        near_stage(space, whole[1:], True, weights, f, partial, layers, tall)
    arrive(masked_copies)
    widen(0)
    widen(layers + 2)
    for space in (1, 2):
        first(space, 1, 1)
        near_stage(space, whole[:1], False, weights, f, partial, layers, tall)
    first(3, 1, layers)
    near_stage(3, whole, True, weights, f, partial, layers, tall)
    arrive(far_copies)
    place_lanes((0, 2), (0, layers + 1))
    for space in range(4):
        first_stage(space, (0, layers + 1, 2), forward, weights, m, mh, c, ch, mz, mhz, f, rs, edges, layers, tall)
        second_stage(space, backward, weights, c, f, rs, partial, sec, b, layers, tall)

    @pl.loop(0, rows // chunk)
    def _(i):
        flat = pl.ds(i * chunk, chunk)
        packed = jnp.zeros((chunk, width), jnp.float32)
        for layer in range(layers + 2):
            for comp in range(3):
                before = pltpu.roll(b[0, layer, comp, flat, :], 1, 1)
                after = pltpu.roll(b[2, layer, comp, flat, :], width - 1, 1)
                own = b[1, layer, comp, flat, :]
                own = own + jnp.where(lane == 0, 0.0, before) + jnp.where(lane == width - 1, 0.0, after)
                sums[layer, comp, flat, :] = own
                spot = comp if layer == 0 else 16 + comp if layer == layers + 1 else 8 + (layer - 1) * 3 + comp
                packed = jnp.where(lane == spot, before[:, :1], packed)
                packed = jnp.where(lane == 24 + spot, after[:, width - 1 :], packed)
        turned[flat, :] = packed
    flipped = turned[...].T
    l_out[...] = flipped[:48].reshape(2, 3, 8, rows)

    last_copies = []
    for side, db in enumerate((1, -1)):
        layer = layers + 1 if db > 0 else 0
        last_copies.append((db, 0, remote(sums.at[layer, two], x_got.at[side], send_x.at[side], got_x.at[side], 0, db)))
    for place, db in enumerate((-1, 0, 1)):
        for side, dg in enumerate((1, -1)):
            last_copies.append((db, dg, remote(l_out.at[side, place], l_got.at[side, place], send_l.at[place, side], got_l.at[place, side], dg, db)))
    start(last_copies)
    sent(lane_copies)
    sent(masked_copies)
    sent(near_copies)
    sent(far_copies)
    arrive(last_copies)
    tail = jnp.zeros((width - 48, rows), jnp.float32)
    turned[...] = jnp.concatenate([l_got[...].reshape(48, rows), tail]).T

    @pl.loop(0, rows // chunk)
    def _(i):
        flat = pl.ds(i * chunk, chunk)
        strips = turned[flat, :]
        for layer in range(layers):
            for comp in range(3):
                total = sums[layer + 1, comp, flat, :]
                if comp > 0 and layer == 0:
                    total = total + x_got[0, comp - 1, flat, :]
                if comp > 0 and layer == layers - 1:
                    total = total + x_got[1, comp - 1, flat, :]
                spot = 8 + layer * 3 + comp
                low, high = strips[:, spot : spot + 1], strips[:, 24 + spot : 25 + spot]
                if layer == layers - 1:
                    low, high = low + strips[:, comp : comp + 1], high + strips[:, 24 + comp : 25 + comp]
                if layer == 0:
                    low, high = low + strips[:, 16 + comp : 17 + comp], high + strips[:, 40 + comp : 41 + comp]
                total = total + jnp.where(lane == 0, low, 0.0) + jnp.where(lane == width - 1, high, 0.0)
                out[comp, layer, flat, :] = total * mask[comp, layer, flat, :].astype(jnp.float32)
    sent(last_copies)


def local(residual, face_mask, conductivity, stencil):
    _, layers, rows, width = residual.shape
    groups = lax.axis_size("grp")
    tall = rows + 2 * PAD
    weights = stencil.reshape(-1)
    smem, vmem = pl.BlockSpec(memory_space=pltpu.SMEM), pl.BlockSpec(memory_space=pltpu.VMEM)
    scratch = lambda *shape: pltpu.VMEM(shape, jnp.float32)
    sems = lambda *shape: pltpu.SemaphoreType.DMA(shape)
    return pl.pallas_call(
        kernel,
        out_shape=jax.ShapeDtypeStruct(residual.shape, jnp.float32),
        in_specs=[smem, vmem, vmem, vmem],
        out_specs=vmem,
        scratch_shapes=[
            scratch(layers + 4, 3, tall, width),
            scratch(layers + 4, 3, tall, width),
            scratch(2, layers + 4, 3, tall, width),
            scratch(2, layers + 4, 3, tall, width),
            scratch(4, layers + 2, rows, width),
            scratch(4, layers + 2, rows, width),
            scratch(4, 3, 3, layers + 2, tall, width),
            scratch(4, layers + 2, 3, rows, width),
            scratch(4, layers, 3, rows, width),
            scratch(3, layers, tall, width),
            scratch(3, layers + 2, 3, rows, width),
            scratch(2, layers, 8, rows),
            scratch(2, layers + 4, 8, rows),
            scratch(groups, 8, rows),
            scratch(3, 4, 8, rows),
            scratch(rows, width),
            scratch(layers + 2, 3, rows, width),
            scratch(2, 2, rows, width),
            scratch(2, 3, 8, rows),
            scratch(2, 3, 8, rows),
            sems(2, 2), sems(2, 2), sems(3, 2), sems(3, 2), sems(3, groups), sems(3, groups),
            sems(3, groups), sems(3, groups), sems(2), sems(2), sems(3, 2), sems(3, 2),
        ],
        compiler_params=pltpu.CompilerParams(
            vmem_limit_bytes=60 * 1024 * 1024, collective_id=0, has_side_effects=True
        ),
        name="correct",
    )(weights, residual, face_mask, conductivity)


def solution(mesh):
    return jax.shard_map(
        local,
        mesh=mesh,
        in_specs=(
            P(None, "blk", None, "grp"),
            P(None, "blk", None, "grp"),
            P("grp", "blk", None, None),
            P(),
        ),
        out_specs=P(None, "blk", None, "grp"),
        check_vma=False,
    )
```
